32 devices in a mesh: ra: 4 (over x, core), rb: 8 (over z, y).
Axes of the slice: x: 2, y: 2, z: 4, core: 2. Of those that a mesh axis runs over, the one named last changes fastest.
Arguments:
- amplitude: bfloat16 [2, 512, 512, 256], P(None, 'ra', 'rb'), may hold values from -6 to 6
- coupling: bfloat16 [6, 256, 256], replicated, may hold values from -0.5 to 0.5
- pattern: int32 [6, 4, 4], replicated, may hold values 0 or 1
- radial: float32 [6, 512, 512], P(None, 'ra', 'rb'), may hold values from -2.4 to 2.4
- first_prop: bfloat16 [2, 512, 512], replicated, may hold values from -0.1875 to 0.1875
- second_prop: bfloat16 [2, 512, 512], replicated, may hold values from -0.1875 to 0.1875
Outputs:
- evolved: bfloat16 [2, 512, 512, 256], P(None, 'ra', 'rb')
The draws below stay inside these ranges and needn't reach their ends.
All inputs are finite; a program needn't handle non-finite values.
Results may differ from the reference program's by a relative error of at most 0.0095.
Values may be sent and summed in bfloat16 or wider, within the bound.
A program may use at most 128 MiB of HBM per device.

```python
import jax
import jax.numpy as jnp
from jax import lax

C = 256
BS = 64
NB = 4
KTERMS = 6
N1 = 512
N2 = 512
STEPS = 2


def place_ends(result, key, least, high):
    spot = [jax.random.randint(jax.random.fold_in(key, axis), (), 0, length) for axis, length in enumerate(result.shape)]
    main_axis = result.shape.index(max(result.shape))
    beside = spot[:main_axis] + [(spot[main_axis] + 1) % result.shape[main_axis]] + spot[main_axis + 1:]
    return result.at[tuple(spot)].set(least).at[tuple(beside)].set(high)


def levels(key, shape, cuts, low, largest):
    factor_of = 1.0
    for dim, parts in cuts:
        heights = jax.random.uniform(jax.random.fold_in(jax.random.fold_in(key, 6), dim), (parts,), jnp.float32, low / len(cuts), largest / len(cuts))
        factor_of = factor_of * jnp.repeat(jnp.exp(heights), shape[dim] // parts).reshape((-1,) + (1,) * (len(shape) - 1 - dim))
    return factor_of


def centred(own_key, shape, scale, bound, shards=(), held_as=jnp.bfloat16):
    factor_of = levels(own_key, shape, shards, -0.22, 0.18) if shards else 1.0
    result = jax.random.normal(own_key, shape, jnp.float32) * scale * factor_of
    return jnp.minimum(jnp.maximum(result, -bound), bound).astype(held_as)


def setup_inputs(seed: int = 0) -> dict:
    splits = jax.random.split(jax.random.key(seed), 7)
    amplitude = centred(splits[0], (2, N1, N2, C), 1.0, 6.0, ((1, 4), (2, 8)))
    coupling = centred(splits[1], (KTERMS, C, C), (C // 2) ** -0.5, 0.5)
    pattern = place_ends((jax.random.randint(splits[2], (KTERMS, NB, NB), 0, 2) < 1).astype(jnp.int32), jax.random.fold_in(splits[2], 1), 0, 1)
    radial = centred(splits[3], (KTERMS, N1, N2), 0.4, 2.4, ((1, 4), (2, 8)), jnp.float32)
    first_prop = centred(splits[4], (2, N1, N1), (2 * N1) ** -0.5, 0.1875)
    second_prop = centred(splits[5], (2, N2, N2), (2 * N2) ** -0.5, 0.1875)
    return dict(amplitude=amplitude, coupling=coupling, pattern=pattern, radial=radial, first_prop=first_prop, second_prop=second_prop)


def spread_mask(pattern):
    blocks = pattern.astype(jnp.float32)
    terms, count = blocks.shape[0], blocks.shape[1]
    spread = jnp.broadcast_to(blocks[:, :, None, :, None], (terms, count, BS, count, BS))
    return spread.reshape(terms, count * BS, count * BS)


def couple(amplitude, coupling, block_mask, radial):
    wide = amplitude.astype(jnp.float32)

    def add_term(multipole, summed):
        weights = coupling[multipole].astype(jnp.float32) * block_mask[multipole]
        applied = jnp.einsum("ij,xabj->xabi", weights, wide)
        return summed + applied * radial[multipole][None, :, :, None]

    coupled = lax.fori_loop(0, KTERMS, add_term, jnp.zeros(amplitude.shape, jnp.float32))
    return jnp.stack([wide[0] + coupled[1], wide[1] - coupled[0]]).astype(jnp.bfloat16)


def along_first(amplitude, propagator):
    wide = amplitude.astype(jnp.float32)
    matrix = propagator.astype(jnp.float32)
    real_part = jnp.einsum("ac,cbi->abi", matrix[0], wide[0]) - jnp.einsum("ac,cbi->abi", matrix[1], wide[1])
    imag_part = jnp.einsum("ac,cbi->abi", matrix[0], wide[1]) + jnp.einsum("ac,cbi->abi", matrix[1], wide[0])
    return jnp.stack([real_part, imag_part]).astype(jnp.bfloat16)


def along_second(amplitude, propagator):
    wide = amplitude.astype(jnp.float32)
    matrix = propagator.astype(jnp.float32)
    real_part = jnp.einsum("bc,aci->abi", matrix[0], wide[0]) - jnp.einsum("bc,aci->abi", matrix[1], wide[1])
    imag_part = jnp.einsum("bc,aci->abi", matrix[0], wide[1]) + jnp.einsum("bc,aci->abi", matrix[1], wide[0])
    return jnp.stack([real_part, imag_part]).astype(jnp.bfloat16)


def reference(amplitude, coupling, pattern, radial, first_prop, second_prop):
    block_mask = spread_mask(pattern)
    for sweep in range(STEPS):
        kicked = couple(amplitude, coupling, block_mask, radial)
        half = along_first(kicked, first_prop)
        amplitude = along_second(half, second_prop)
    return amplitude
```

```python
import functools

import jax
import jax.numpy as jnp
from jax import lax
from jax.experimental import pallas as pl
from jax.experimental.pallas import tpu as pltpu
from jax.sharding import PartitionSpec as P

KTERMS = 6
STEPS = 2
LANES = 128
TILE = 16


def complex_rows(matrix, piece):
    form = "ac,cqw->aqw"
    real_part = jnp.einsum(
        form, matrix[0], piece[0], preferred_element_type=jnp.float32
    ) - jnp.einsum(form, matrix[1], piece[1], preferred_element_type=jnp.float32)
    imag_part = jnp.einsum(
        form, matrix[0], piece[1], preferred_element_type=jnp.float32
    ) + jnp.einsum(form, matrix[1], piece[0], preferred_element_type=jnp.float32)
    return jnp.stack([real_part, imag_part]).astype(jnp.bfloat16)


def masked_weights(coupling, pattern):
    channels = coupling.shape[1]
    count = pattern.shape[1]
    block_size = channels // count
    spread = jnp.broadcast_to(
        pattern[:, :, None, :, None], (KTERMS, count, block_size, count, block_size)
    )
    return coupling * spread.reshape(KTERMS, channels, channels).astype(jnp.bfloat16)


def plain(amplitude, coupling, pattern, radial, first_prop, second_prop):
    first_rows, second_rows, channels = (amplitude.shape[1], amplitude.shape[2], amplitude.shape[3])
    cells = first_rows * second_rows
    groups_a = lax.axis_size("ra")
    groups_b = lax.axis_size("rb")
    width_a = channels // groups_a
    width_b = channels // groups_b
    weights = masked_weights(coupling, pattern)
    radial_cells = radial.reshape(KTERMS, cells).T
    for sweep in range(STEPS):
        flat = amplitude.reshape(2 * cells, channels)
        applied = jnp.einsum("mj,kij->mki", flat, weights, preferred_element_type=jnp.float32)
        applied = applied.reshape(2, cells, KTERMS, channels)
        coupled = jnp.sum(applied * radial_cells[None, :, :, None], axis=2)
        wide = amplitude.reshape(2, cells, channels).astype(jnp.float32)
        kicked = jnp.stack([wide[0] + coupled[1], wide[1] - coupled[0]]).astype(jnp.bfloat16)
        grouped = kicked.reshape(2, first_rows, second_rows, groups_a, width_a)
        grouped = grouped.transpose(0, 1, 3, 2, 4).reshape(
            2, first_rows, groups_a, second_rows * width_a
        )
        half = complex_rows(
            first_prop, lax.all_to_all(grouped, "ra", split_axis=2, concat_axis=1, tiled=True)
        )
        restored = lax.all_to_all(half, "ra", split_axis=1, concat_axis=2, tiled=True)
        restored = restored.reshape(2, first_rows, groups_a, second_rows, width_a)
        restored = restored.transpose(0, 1, 3, 2, 4).reshape(
            2, first_rows, second_rows, groups_b, width_b
        )
        regrouped = restored.transpose(0, 2, 3, 1, 4).reshape(
            2, second_rows, groups_b, first_rows * width_b
        )
        moved = complex_rows(
            second_prop, lax.all_to_all(regrouped, "rb", split_axis=2, concat_axis=1, tiled=True)
        )
        settled = lax.all_to_all(moved, "rb", split_axis=1, concat_axis=2, tiled=True)
        settled = settled.reshape(2, second_rows, groups_b, first_rows, width_b)
        amplitude = settled.transpose(0, 3, 1, 2, 4).reshape(2, first_rows, second_rows, channels)
    return amplitude


def prop_kernel(turned, n_in, n_out, mat_ref, *refs):
    ins, outs, rest = refs[:n_in], refs[n_in:n_in + n_out], refs[n_in + n_out:]
    depth = mat_ref.shape[1]
    outer = ins[0].shape[1]
    rows = depth // n_out
    step = pl.program_id(0)

    def one(o, carry):
        real = jnp.concatenate([r[0, o] for r in ins], axis=0)
        imag = jnp.concatenate([r[1, o] for r in ins], axis=0)
        res = jnp.dot(
            mat_ref[0], jnp.concatenate([real, imag], axis=1), preferred_element_type=jnp.float32
        ) + jnp.dot(
            mat_ref[1], jnp.concatenate([-imag, real], axis=1), preferred_element_type=jnp.float32
        )
        if turned:
            for p in range(2):
                rest[0][p, pl.ds(step * outer + o, depth, stride=TILE), :] = res[:, p * LANES:(p + 1) * LANES]
        else:
            for p in range(2):
                for s in range(n_out):
                    outs[s][p, o] = res[s * rows:(s + 1) * rows, p * LANES:(p + 1) * LANES].astype(jnp.bfloat16)
        return carry

    lax.fori_loop(0, outer, one, 0)
    if turned:
        @pl.when(step == pl.num_programs(0) - 1)
        def _():
            span = rows * TILE
            for p in range(2):
                for s in range(n_out):
                    outs[s][p] = rest[0][p, s * span:(s + 1) * span, :].reshape(rows, TILE, LANES).astype(jnp.bfloat16)


def propagate(matrix, pieces, place, n_out, turned):
    depth = matrix.shape[1]
    rows = depth // n_out
    outer = 4
    parts = TILE // outer
    in_specs = [pl.BlockSpec(matrix.shape, lambda g: (0, 0, 0))] + [
        pl.BlockSpec((2, outer, p.shape[2], LANES), lambda g: (0, place * parts + g, 0, 0)) for p in pieces
    ]
    if turned:
        shape = (2, rows, TILE, LANES)
        out_specs = [pl.BlockSpec(shape, lambda g: (0, 0, 0, 0))] * n_out
        scratch = [pltpu.VMEM((2, depth * TILE, LANES), jnp.float32)]
    else:
        shape = (2, TILE, rows, LANES)
        out_specs = [pl.BlockSpec((2, outer, rows, LANES), lambda g: (0, g, 0, 0))] * n_out
        scratch = []
    return pl.pallas_call(
        functools.partial(prop_kernel, turned, len(pieces), n_out),
        grid=(parts,),
        in_specs=in_specs,
        out_specs=out_specs,
        out_shape=[jax.ShapeDtypeStruct(shape, jnp.bfloat16)] * n_out,
        scratch_shapes=scratch,
        cost_estimate=pl.CostEstimate(
            flops=8 * depth * depth * TILE * LANES, bytes_accessed=8 * depth * TILE * LANES, transcendentals=0
        ),
        compiler_params=pltpu.CompilerParams(vmem_limit_bytes=56 * 2**20),
    )(matrix, *pieces)


def kick_rows(planes, old, weights, factor):
    coupled = []
    for p in range(2):
        applied = jnp.dot(planes[p], weights, preferred_element_type=jnp.float32)
        total = applied[:, :LANES] * factor[:, 0:1]
        for k in range(1, KTERMS):
            total = total + applied[:, k * LANES:(k + 1) * LANES] * factor[:, k:k + 1]
        coupled.append(total)
    return old[0].astype(jnp.float32) + coupled[1], old[1].astype(jnp.float32) - coupled[0]


def kick_turned_kernel(where_ref, amp_ref, old_ref, weights_ref, factor_ref, out_ref):
    a_rows, b_rows = amp_ref.shape[1], amp_ref.shape[2]
    count = a_rows * b_rows
    planes = [amp_ref[p].reshape(count, amp_ref.shape[3]) for p in range(2)]
    old = [old_ref[p].reshape(count, LANES) for p in range(2)]
    result = kick_rows(planes, old, weights_ref[...], factor_ref[...].reshape(count, KTERMS))
    for p in range(2):
        out_ref[p] = jnp.swapaxes(result[p].reshape(a_rows, b_rows, LANES), 0, 1).astype(jnp.bfloat16)


def kick_turned(amplitude, weights, factor, where):
    a_rows, channels = amplitude.shape[1], amplitude.shape[3]
    spec = pltpu.PrefetchScalarGridSpec(
        num_scalar_prefetch=1,
        grid=(a_rows // TILE,),
        in_specs=[
            pl.BlockSpec((2, TILE, TILE, channels), lambda g, w: (0, g, w[0], 0)),
            pl.BlockSpec((2, TILE, TILE, LANES), lambda g, w: (0, g, w[0], w[1])),
            pl.BlockSpec(weights.shape, lambda g, w: (0, 0)),
            pl.BlockSpec((TILE, TILE, KTERMS), lambda g, w: (g, w[0], 0)),
        ],
        out_specs=pl.BlockSpec((2, TILE, TILE, LANES), lambda g, w: (0, 0, g, 0)),
    )
    return pl.pallas_call(
        kick_turned_kernel,
        grid_spec=spec,
        out_shape=jax.ShapeDtypeStruct((2, TILE, a_rows, LANES), jnp.bfloat16),
        cost_estimate=pl.CostEstimate(
            flops=4 * TILE * a_rows * channels * KTERMS * LANES,
            bytes_accessed=4 * TILE * a_rows * (channels + 2 * LANES), transcendentals=0,
        ),
    )(where, amplitude, amplitude, weights, factor)


def kick_pair_kernel(own_ref, other_ref, weights_ref, factor_ref, own_out, other_out):
    halves = [[ref[p, 0] for p in range(2)] for ref in (own_ref, other_ref)]
    planes = [jnp.concatenate([halves[0][p], halves[1][p]], axis=1) for p in range(2)]
    factor = factor_ref[0]
    for s, out in enumerate((own_out, other_out)):
        result = kick_rows(planes, halves[s], weights_ref[s], factor)
        for p in range(2):
            out[p, 0] = result[p].astype(jnp.bfloat16)


def kick_pair(own, other, weights, factor, place):
    a_rows, b_rows = own.shape[1], own.shape[2]
    block = pl.BlockSpec((2, 1, b_rows, LANES), lambda g: (0, g, 0, 0))
    shape = jax.ShapeDtypeStruct(own.shape, jnp.bfloat16)
    return pl.pallas_call(
        kick_pair_kernel,
        grid=(a_rows,),
        in_specs=[
            block, block,
            pl.BlockSpec(weights.shape, lambda g: (0, 0, 0)),
            pl.BlockSpec((1, b_rows, KTERMS), lambda g: (place * a_rows + g, 0, 0)),
        ],
        out_specs=[block, block],
        out_shape=[shape, shape],
        cost_estimate=pl.CostEstimate(
            flops=4 * a_rows * b_rows * 4 * LANES * KTERMS * LANES,
            bytes_accessed=16 * a_rows * b_rows * LANES, transcendentals=0,
        ),
    )(own, other, weights, factor)


def join_kernel(where_ref, piece_ref, *refs):
    refs[-1][...] = piece_ref[...]


def join(piece, into, where, shape):
    a_rows = piece.shape[1]
    step = 32
    have = into is not None
    spec = pltpu.PrefetchScalarGridSpec(
        num_scalar_prefetch=1,
        grid=(a_rows // step,),
        in_specs=[pl.BlockSpec((2, step, TILE, LANES), lambda g, w: (0, g, 0, 0))]
        + ([pl.BlockSpec(memory_space=pl.ANY)] if have else []),
        out_specs=pl.BlockSpec((2, step, TILE, LANES), lambda g, w: (0, g, w[0], w[1])),
    )
    return pl.pallas_call(
        join_kernel,
        grid_spec=spec,
        out_shape=jax.ShapeDtypeStruct(shape, jnp.bfloat16),
        input_output_aliases={2: 0} if have else {},
    )(where, piece, *((into,) if have else ()))


def picks(index):
    full = index.shape[0]
    return (index[:, None] == jnp.arange(full)[None, :]).astype(jnp.bfloat16)


def arranged(matrix, rows, columns):
    first = jnp.einsum("rs,xst->xrt", picks(rows), matrix, preferred_element_type=jnp.float32)
    return jnp.einsum(
        "xrt,ct->xrc", first.astype(jnp.bfloat16), picks(columns), preferred_element_type=jnp.float32
    ).astype(jnp.bfloat16)


def on_device(amplitude, coupling, pattern, radial, first_prop, second_prop):
    a_rows, b_rows, channels = amplitude.shape[1:]
    n_a, n_b = first_prop.shape[1], second_prop.shape[1]
    ra, rb = lax.axis_size("ra"), lax.axis_size("rb")
    inner = ra // 2
    far = inner * rb
    a_far, b_far = n_a // far, n_b // far
    fits = (
        channels == 2 * LANES and ra % 2 == 0 and a_rows % TILE == 0
        and a_far % TILE == 0 and b_far % TILE == 0 and far & (far - 1) == 0
        and far <= 16
    )
    if not fits:
        return plain(amplitude, coupling, pattern, radial, first_prop, second_prop)

    at_a, at_b = lax.axis_index("ra"), lax.axis_index("rb")
    x, core = at_a // inner, at_a % inner
    spot = core * rb + at_b
    axes = ("ra", "rb")
    index = lambda ia, ib: ia * rb + ib

    def send_near(piece, s):
        if s == 0:
            return piece
        return lax.ppermute(piece, axes, [(index(i, j), index(i ^ s, j)) for i in range(ra) for j in range(rb)])

    def send_far(piece, s):
        if s == 0:
            return piece
        pairs = []
        for i in range(ra):
            for j in range(rb):
                to = ((i % inner) * rb + j) ^ s
                pairs.append((index(i, j), index(i // inner * inner + to // rb, to % rb)))
        return lax.ppermute(piece, axes, pairs)

    ia, ib = jnp.arange(n_a), jnp.arange(n_b)
    peer = spot ^ (ia // a_far)
    t = ia % a_far
    half_far = a_far // 2
    far_a = (t // half_far) * (n_a // 2) + (peer // rb) * a_rows + (peer % rb) * half_far + t % half_far
    peer = spot ^ (ib // b_far)
    far_b = (peer % rb) * b_rows + (peer // rb) * b_far + ib % b_far
    near_a = (at_a ^ (ia // a_rows)) * a_rows + ia % a_rows
    half_b = n_b // 2
    near_b = (x ^ (ib // half_b)) * half_b + ib % half_b

    first_out = arranged(first_prop, far_a, near_a)
    second_in = arranged(second_prop, near_b, far_b)
    second_out = arranged(second_prop, far_b, near_b)
    first_back = arranged(first_prop, near_a, far_a)

    weights = masked_weights(coupling, pattern).reshape(KTERMS, 2, LANES, channels)
    weights = weights.transpose(1, 3, 0, 2).reshape(2, channels, KTERMS * LANES)
    weights = jnp.where(x == 0, weights, weights[::-1])
    turned = weights.reshape(2, 2, LANES, KTERMS * LANES)
    turned = jnp.where(x == 0, turned, turned[:, ::-1]).reshape(weights.shape)

    near_radial = radial.transpose(1, 2, 0)
    wide = lax.all_to_all(radial, "rb", split_axis=1, concat_axis=2, tiled=True)
    split = wide.reshape(KTERMS, half_far, 2, half_b)
    keep = jnp.where(x == 0, split[:, :, 0], split[:, :, 1])
    give = jnp.where(x == 0, split[:, :, 1], split[:, :, 0])
    got = send_near(give, inner)
    low = jnp.where(x == 0, keep, got)
    high = jnp.where(x == 0, got, keep)
    far_radial = jnp.concatenate([low, high], axis=1).transpose(1, 2, 0)

    b_parts, a_parts = b_far // TILE, a_far // TILE

    def block_of(s, part):
        return jnp.stack([(core ^ (s % inner)) * b_parts + part, x ^ (s // inner)]).astype(jnp.int32)

    halves = []
    for part in range(b_parts):
        pieces = []
        for s in reversed(range(ra)):
            kicked = kick_turned(amplitude, weights[s // inner], near_radial, block_of(s, part))
            pieces.append(send_near(kicked, s))
        pieces = pieces[::-1]
        half = propagate(first_out, pieces, 0, far, True)
        halves.append([send_far(h, s) for s, h in enumerate(half)])
    gathered = [halves[part][s] for s in range(far) for part in range(b_parts)]

    back = []
    for part in range(a_parts):
        own, other = propagate(second_in, gathered, part, 2, False)
        other = send_near(other, inner)
        own, other = kick_pair(own, other, turned, far_radial, part)
        other = send_near(other, inner)
        half = propagate(second_out, [own, other], 0, far, True)
        back.append([send_far(h, s) for s, h in enumerate(half)])
    gathered = [back[part][s] for s in range(far) for part in range(a_parts)]

    result = None
    for part in range(b_parts):
        moved = propagate(first_back, gathered, part, ra, True)
        for s, piece in enumerate(moved):
            result = join(send_near(piece, s), result, block_of(s, part), amplitude.shape)
    return result


def solution(mesh):
    return jax.shard_map(
        on_device,
        mesh=mesh,
        in_specs=(P(None, "ra", "rb", None), P(), P(), P(None, "ra", "rb"), P(), P()),
        out_specs=P(None, "ra", "rb", None),
        check_vma=False,
    )
```

```python
import functools

import jax
import jax.numpy as jnp
from jax import lax
from jax.experimental import pallas as pl
from jax.experimental.pallas import tpu as pltpu
from jax.sharding import PartitionSpec as P

KTERMS = 6
STEPS = 2
LANES = 128
TILE = 16


def complex_rows(matrix, piece):
    form = "ac,cqw->aqw"
    real_part = jnp.einsum(
        form, matrix[0], piece[0], preferred_element_type=jnp.float32
    ) - jnp.einsum(form, matrix[1], piece[1], preferred_element_type=jnp.float32)
    imag_part = jnp.einsum(
        form, matrix[0], piece[1], preferred_element_type=jnp.float32
    ) + jnp.einsum(form, matrix[1], piece[0], preferred_element_type=jnp.float32)
    return jnp.stack([real_part, imag_part]).astype(jnp.bfloat16)


def masked_weights(coupling, pattern):
    channels = coupling.shape[1]
    count = pattern.shape[1]
    block_size = channels // count
    spread = jnp.broadcast_to(
        pattern[:, :, None, :, None], (KTERMS, count, block_size, count, block_size)
    )
    return coupling * spread.reshape(KTERMS, channels, channels).astype(jnp.bfloat16)


def plain(amplitude, coupling, pattern, radial, first_prop, second_prop):
    first_rows, second_rows, channels = (amplitude.shape[1], amplitude.shape[2], amplitude.shape[3])
    cells = first_rows * second_rows
    groups_a = lax.axis_size("ra")
    groups_b = lax.axis_size("rb")
    width_a = channels // groups_a
    width_b = channels // groups_b
    weights = masked_weights(coupling, pattern)
    radial_cells = radial.reshape(KTERMS, cells).T
    for sweep in range(STEPS):
        flat = amplitude.reshape(2 * cells, channels)
        applied = jnp.einsum("mj,kij->mki", flat, weights, preferred_element_type=jnp.float32)
        applied = applied.reshape(2, cells, KTERMS, channels)
        coupled = jnp.sum(applied * radial_cells[None, :, :, None], axis=2)
        wide = amplitude.reshape(2, cells, channels).astype(jnp.float32)
        kicked = jnp.stack([wide[0] + coupled[1], wide[1] - coupled[0]]).astype(jnp.bfloat16)
        grouped = kicked.reshape(2, first_rows, second_rows, groups_a, width_a)
        grouped = grouped.transpose(0, 1, 3, 2, 4).reshape(
            2, first_rows, groups_a, second_rows * width_a
        )
        half = complex_rows(
            first_prop, lax.all_to_all(grouped, "ra", split_axis=2, concat_axis=1, tiled=True)
        )
        restored = lax.all_to_all(half, "ra", split_axis=1, concat_axis=2, tiled=True)
        restored = restored.reshape(2, first_rows, groups_a, second_rows, width_a)
        restored = restored.transpose(0, 1, 3, 2, 4).reshape(
            2, first_rows, second_rows, groups_b, width_b
        )
        regrouped = restored.transpose(0, 2, 3, 1, 4).reshape(
            2, second_rows, groups_b, first_rows * width_b
        )
        moved = complex_rows(
            second_prop, lax.all_to_all(regrouped, "rb", split_axis=2, concat_axis=1, tiled=True)
        )
        settled = lax.all_to_all(moved, "rb", split_axis=1, concat_axis=2, tiled=True)
        settled = settled.reshape(2, second_rows, groups_b, first_rows, width_b)
        amplitude = settled.transpose(0, 3, 1, 2, 4).reshape(2, first_rows, second_rows, channels)
    return amplitude


def prop_kernel(turned, n_in, n_out, mat_ref, *refs):
    ins, outs, rest = refs[:n_in], refs[n_in:n_in + n_out], refs[n_in + n_out:]
    depth = mat_ref.shape[1]
    outer = ins[0].shape[1]
    rows = depth // n_out
    step = pl.program_id(0)

    def one(o, carry):
        real = jnp.concatenate([r[0, o] for r in ins], axis=0)
        imag = jnp.concatenate([r[1, o] for r in ins], axis=0)
        res = jnp.dot(
            mat_ref[0], jnp.concatenate([real, imag], axis=1), preferred_element_type=jnp.float32
        ) + jnp.dot(
            mat_ref[1], jnp.concatenate([-imag, real], axis=1), preferred_element_type=jnp.float32
        )
        if turned:
            for p in range(2):
                rest[0][p, pl.ds(step * outer + o, depth, stride=TILE), :] = res[:, p * LANES:(p + 1) * LANES]
        else:
            for p in range(2):
                for s in range(n_out):
                    outs[s][p, o] = res[s * rows:(s + 1) * rows, p * LANES:(p + 1) * LANES].astype(jnp.bfloat16)
        return carry

    lax.fori_loop(0, outer, one, 0)
    if turned:
        @pl.when(step == pl.num_programs(0) - 1)
        def _():
            span = rows * TILE
            for p in range(2):
                for s in range(n_out):
                    outs[s][p] = rest[0][p, s * span:(s + 1) * span, :].reshape(rows, TILE, LANES).astype(jnp.bfloat16)


def propagate(matrix, pieces, place, n_out, turned):
    depth = matrix.shape[1]
    rows = depth // n_out
    outer = 4
    parts = TILE // outer
    in_specs = [pl.BlockSpec(matrix.shape, lambda g: (0, 0, 0))] + [
        pl.BlockSpec((2, outer, p.shape[2], LANES), lambda g: (0, place * parts + g, 0, 0)) for p in pieces
    ]
    if turned:
        shape = (2, rows, TILE, LANES)
        out_specs = [pl.BlockSpec(shape, lambda g: (0, 0, 0, 0))] * n_out
        scratch = [pltpu.VMEM((2, depth * TILE, LANES), jnp.float32)]
    else:
        shape = (2, TILE, rows, LANES)
        out_specs = [pl.BlockSpec((2, outer, rows, LANES), lambda g: (0, g, 0, 0))] * n_out
        scratch = []
    return pl.pallas_call(
        functools.partial(prop_kernel, turned, len(pieces), n_out),
        grid=(parts,),
        in_specs=in_specs,
        out_specs=out_specs,
        out_shape=[jax.ShapeDtypeStruct(shape, jnp.bfloat16)] * n_out,
        scratch_shapes=scratch,
        cost_estimate=pl.CostEstimate(
            flops=8 * depth * depth * TILE * LANES, bytes_accessed=8 * depth * TILE * LANES, transcendentals=0
        ),
        compiler_params=pltpu.CompilerParams(vmem_limit_bytes=56 * 2**20),
    )(matrix, *pieces)


def kick_rows(planes, old, weights, factor):
    coupled = []
    for p in range(2):
        applied = jnp.dot(planes[p], weights, preferred_element_type=jnp.float32)
        total = applied[:, :LANES] * factor[:, 0:1]
        for k in range(1, KTERMS):
            total = total + applied[:, k * LANES:(k + 1) * LANES] * factor[:, k:k + 1]
        coupled.append(total)
    return old[0].astype(jnp.float32) + coupled[1], old[1].astype(jnp.float32) - coupled[0]


def kick_turned_kernel(where_ref, amp_ref, weights_ref, factor_ref, *outs):
    a_rows, b_rows = amp_ref.shape[1], amp_ref.shape[2]
    count = a_rows * b_rows
    planes = [amp_ref[p].reshape(count, amp_ref.shape[3]) for p in range(2)]
    factor = factor_ref[...].reshape(count, KTERMS)
    for s in range(2):
        low = where_ref[1] == s
        old = [jnp.where(low, p[:, :LANES], p[:, LANES:]) for p in planes]
        result = kick_rows(planes, old, weights_ref[s], factor)
        for p in range(2):
            outs[s][p] = jnp.swapaxes(result[p].reshape(a_rows, b_rows, LANES), 0, 1).astype(jnp.bfloat16)


def kick_turned(amplitude, weights, factor, where):
    a_rows, channels = amplitude.shape[1], amplitude.shape[3]
    shape = jax.ShapeDtypeStruct((2, TILE, a_rows, LANES), jnp.bfloat16)
    spec = pltpu.PrefetchScalarGridSpec(
        num_scalar_prefetch=1,
        grid=(a_rows // TILE,),
        in_specs=[
            pl.BlockSpec((2, TILE, TILE, channels), lambda g, w: (0, g, w[0], 0)),
            pl.BlockSpec(weights.shape, lambda g, w: (0, 0, 0)),
            pl.BlockSpec((TILE, TILE, KTERMS), lambda g, w: (g, w[0], 0)),
        ],
        out_specs=[pl.BlockSpec((2, TILE, TILE, LANES), lambda g, w: (0, 0, g, 0))] * 2,
    )
    return pl.pallas_call(
        kick_turned_kernel,
        grid_spec=spec,
        out_shape=[shape, shape],
        cost_estimate=pl.CostEstimate(
            flops=8 * TILE * a_rows * channels * KTERMS * LANES,
            bytes_accessed=8 * TILE * a_rows * channels, transcendentals=0,
        ),
    )(where, amplitude, weights, factor)


def kick_pair_kernel(own_ref, other_ref, weights_ref, factor_ref, own_out, other_out):
    halves = [[ref[p, 0] for p in range(2)] for ref in (own_ref, other_ref)]
    planes = [jnp.concatenate([halves[0][p], halves[1][p]], axis=1) for p in range(2)]
    factor = factor_ref[0]
    for s, out in enumerate((own_out, other_out)):
        result = kick_rows(planes, halves[s], weights_ref[s], factor)
        for p in range(2):
            out[p, 0] = result[p].astype(jnp.bfloat16)


def kick_pair(own, other, weights, factor, place):
    a_rows, b_rows = own.shape[1], own.shape[2]
    block = pl.BlockSpec((2, 1, b_rows, LANES), lambda g: (0, g, 0, 0))
    shape = jax.ShapeDtypeStruct(own.shape, jnp.bfloat16)
    return pl.pallas_call(
        kick_pair_kernel,
        grid=(a_rows,),
        in_specs=[
            block, block,
            pl.BlockSpec(weights.shape, lambda g: (0, 0, 0)),
            pl.BlockSpec((1, b_rows, KTERMS), lambda g: (place * a_rows + g, 0, 0)),
        ],
        out_specs=[block, block],
        out_shape=[shape, shape],
        cost_estimate=pl.CostEstimate(
            flops=4 * a_rows * b_rows * 4 * LANES * KTERMS * LANES,
            bytes_accessed=16 * a_rows * b_rows * LANES, transcendentals=0,
        ),
    )(own, other, weights, factor)


def join_kernel(where_ref, own_ref, other_ref, *refs):
    low = where_ref[1] == 0
    own, other = own_ref[...], other_ref[...]
    refs[-1][:, :, :, :LANES] = jnp.where(low, own, other)
    refs[-1][:, :, :, LANES:] = jnp.where(low, other, own)


def join(own, other, into, where, shape):
    a_rows = own.shape[1]
    step = 32
    have = into is not None
    spec = pltpu.PrefetchScalarGridSpec(
        num_scalar_prefetch=1,
        grid=(a_rows // step,),
        in_specs=[pl.BlockSpec((2, step, TILE, LANES), lambda g, w: (0, g, 0, 0))] * 2
        + ([pl.BlockSpec(memory_space=pl.ANY)] if have else []),
        out_specs=pl.BlockSpec((2, step, TILE, 2 * LANES), lambda g, w: (0, g, w[0], 0)),
    )
    return pl.pallas_call(
        join_kernel,
        grid_spec=spec,
        out_shape=jax.ShapeDtypeStruct(shape, jnp.bfloat16),
        input_output_aliases={3: 0} if have else {},
        cost_estimate=pl.CostEstimate(flops=0, bytes_accessed=8 * own.size, transcendentals=0),
    )(where, own, other, *((into,) if have else ()))


def picks(index):
    full = index.shape[0]
    return (index[:, None] == jnp.arange(full)[None, :]).astype(jnp.bfloat16)


def arranged(matrix, rows, columns):
    first = jnp.einsum("rs,xst->xrt", picks(rows), matrix, preferred_element_type=jnp.float32)
    return jnp.einsum(
        "xrt,ct->xrc", first.astype(jnp.bfloat16), picks(columns), preferred_element_type=jnp.float32
    ).astype(jnp.bfloat16)


def on_device(amplitude, coupling, pattern, radial, first_prop, second_prop):
    a_rows, b_rows, channels = amplitude.shape[1:]
    n_a, n_b = first_prop.shape[1], second_prop.shape[1]
    ra, rb = lax.axis_size("ra"), lax.axis_size("rb")
    far = ra // 2 * rb
    a_far, b_far = n_a // far, n_b // far
    fits = (
        channels == 2 * LANES and ra % 2 == 0 and a_rows % TILE == 0
        and a_far % TILE == 0 and b_far % TILE == 0 and far & (far - 1) == 0
        and far <= 16
    )
    if not fits:
        return plain(amplitude, coupling, pattern, radial, first_prop, second_prop)

    at_a, at_b = lax.axis_index("ra"), lax.axis_index("rb")
    outer, half = at_a // 2, at_a % 2
    spot = outer * rb + at_b
    axes = ("ra", "rb")
    index = lambda ia, ib: ia * rb + ib

    def send_near(piece, s):
        if s == 0:
            return piece
        return lax.ppermute(piece, axes, [(index(i, j), index(i ^ s, j)) for i in range(ra) for j in range(rb)])

    def send_far(piece, s):
        if s == 0:
            return piece
        pairs = []
        for i in range(ra):
            for j in range(rb):
                to = ((i // 2) * rb + j) ^ s
                pairs.append((index(i, j), index((to // rb) * 2 + i % 2, to % rb)))
        return lax.ppermute(piece, axes, pairs)

    half_far, half_rb, half_b = a_far // 2, rb // 2, n_b // 2
    got = []
    for u in range(rb):
        pairs = []
        for i in range(ra):
            for j in range(rb):
                to = ((i % 2) * half_rb + j % half_rb) ^ u
                pairs.append((index(i, j), index(i // 2 * 2 + j // half_rb, to)))
        to = (half * half_rb + at_b % half_rb) ^ u
        piece = lax.dynamic_slice_in_dim(radial, to * half_far, half_far, axis=1)
        got.append(lax.ppermute(piece, axes, pairs))

    ia, ib = jnp.arange(n_a), jnp.arange(n_b)
    peer = spot ^ (ia // a_far)
    t = ia % a_far
    far_a = (peer // rb) * 2 * a_rows + (t // half_far) * a_rows + (peer % rb) * half_far + t % half_far
    peer = spot ^ (ib // b_far)
    far_b = (peer % rb) * b_rows + (peer // rb) * b_far + ib % b_far
    near_a = (at_a ^ (ia // a_rows)) * a_rows + ia % a_rows
    near_b = (half ^ (ib // half_b)) * half_b + ib % half_b

    first_out = arranged(first_prop, far_a, near_a)
    second_in = arranged(second_prop, near_b, far_b)
    second_out = arranged(second_prop, far_b, near_b)
    first_back = arranged(first_prop, near_a, far_a)

    weights = masked_weights(coupling, pattern).reshape(KTERMS, 2, LANES, channels)
    weights = weights.transpose(1, 3, 0, 2).reshape(2, channels, KTERMS * LANES)
    weights = jnp.where(half == 0, weights, weights[::-1])
    near_radial = radial.transpose(1, 2, 0)

    b_parts, a_parts = b_far // TILE, a_far // TILE

    def block_of(s, part):
        return jnp.stack([(outer ^ s) * b_parts + part, half]).astype(jnp.int32)

    halves = []
    ready = weights
    for part in range(b_parts):
        pieces = [None] * ra
        for s in reversed(range(ra // 2)):
            kicked = kick_turned(amplitude, ready, near_radial, block_of(s, part))
            if part == 0 and s == ra // 2 - 1:
                ready, got = lax.optimization_barrier((weights, got))
            for h in (1, 0):
                pieces[2 * s + h] = send_near(kicked[h], 2 * s + h)
        spread = propagate(first_out, pieces, 0, far, True)
        halves.append([send_far(h, s) for s, h in enumerate(spread)])
    gathered = [halves[part][s] for s in range(far) for part in range(b_parts)]

    turned = weights.reshape(2, 2, LANES, KTERMS * LANES)
    turned = jnp.where(half == 0, turned, turned[:, ::-1]).reshape(weights.shape)
    ordered = jnp.stack(got)
    for bit in range(rb.bit_length() - 1):
        pairs = ordered.reshape(rb >> (bit + 1), 2, 1 << bit, *got[0].shape)
        pairs = jnp.where((at_b >> bit) % 2 == 0, pairs, pairs[:, ::-1])
        ordered = pairs.reshape(rb, *got[0].shape)
    ordered = ordered.reshape(2, half_rb, KTERMS, half_far, b_rows)
    far_radial = ordered.transpose(0, 3, 1, 4, 2).reshape(a_far, half_b, KTERMS)
    back = []
    for part in range(a_parts):
        own, other = propagate(second_in, gathered, part, 2, False)
        other = send_near(other, 1)
        own, other = kick_pair(own, other, turned, far_radial, part)
        other = send_near(other, 1)
        spread = propagate(second_out, [own, other], 0, far, True)
        back.append([send_far(h, s) for s, h in enumerate(spread)])
    gathered = [back[part][s] for s in range(far) for part in range(a_parts)]

    result = None
    for part in range(b_parts):
        moved = propagate(first_back, gathered, part, ra, True)
        moved = [send_near(piece, s) for s, piece in enumerate(moved)]
        for s in range(ra // 2):
            result = join(moved[2 * s], moved[2 * s + 1], result, block_of(s, part), amplitude.shape)
    return result


def solution(mesh):
    return jax.shard_map(
        on_device,
        mesh=mesh,
        in_specs=(P(None, "ra", "rb", None), P(), P(), P(None, "ra", "rb"), P(), P()),
        out_specs=P(None, "ra", "rb", None),
        check_vma=False,
    )
```

```python
import functools

import jax
import jax.numpy as jnp
from jax import lax
from jax.experimental import pallas as pl
from jax.experimental.pallas import tpu as pltpu
from jax.sharding import PartitionSpec as P


KTERMS = 6
STEPS = 2
LANES = 128
TILE = 16


def complex_rows(matrix, piece):
    form = "ac,cqw->aqw"
    real_part = jnp.einsum(
        form, matrix[0], piece[0], preferred_element_type=jnp.float32
    ) - jnp.einsum(form, matrix[1], piece[1], preferred_element_type=jnp.float32)
    imag_part = jnp.einsum(
        form, matrix[0], piece[1], preferred_element_type=jnp.float32
    ) + jnp.einsum(form, matrix[1], piece[0], preferred_element_type=jnp.float32)
    return jnp.stack([real_part, imag_part]).astype(jnp.bfloat16)


def masked_weights(coupling, pattern):
    channels = coupling.shape[1]
    count = pattern.shape[1]
    block_size = channels // count
    spread = jnp.broadcast_to(
        pattern[:, :, None, :, None], (KTERMS, count, block_size, count, block_size)
    )
    return coupling * spread.reshape(KTERMS, channels, channels).astype(jnp.bfloat16)


def plain(amplitude, coupling, pattern, radial, first_prop, second_prop):
    first_rows, second_rows, channels = (amplitude.shape[1], amplitude.shape[2], amplitude.shape[3])
    cells = first_rows * second_rows
    groups_a = lax.axis_size("ra")
    groups_b = lax.axis_size("rb")
    width_a = channels // groups_a
    width_b = channels // groups_b
    weights = masked_weights(coupling, pattern)
    radial_cells = radial.reshape(KTERMS, cells).T
    for _ in range(STEPS):
        flat = amplitude.reshape(2 * cells, channels)
        applied = jnp.einsum("mj,kij->mki", flat, weights, preferred_element_type=jnp.float32)
        applied = applied.reshape(2, cells, KTERMS, channels)
        coupled = jnp.sum(applied * radial_cells[None, :, :, None], axis=2)
        wide = amplitude.reshape(2, cells, channels).astype(jnp.float32)
        kicked = jnp.stack([wide[0] + coupled[1], wide[1] - coupled[0]]).astype(jnp.bfloat16)
        grouped = kicked.reshape(2, first_rows, second_rows, groups_a, width_a)
        grouped = grouped.transpose(0, 1, 3, 2, 4).reshape(
            2, first_rows, groups_a, second_rows * width_a
        )
        half = complex_rows(
            first_prop, lax.all_to_all(grouped, "ra", split_axis=2, concat_axis=1, tiled=True)
        )
        restored = lax.all_to_all(half, "ra", split_axis=1, concat_axis=2, tiled=True)
        restored = restored.reshape(2, first_rows, groups_a, second_rows, width_a)
        restored = restored.transpose(0, 1, 3, 2, 4).reshape(
            2, first_rows, second_rows, groups_b, width_b
        )
        regrouped = restored.transpose(0, 2, 3, 1, 4).reshape(
            2, second_rows, groups_b, first_rows * width_b
        )
        moved = complex_rows(
            second_prop, lax.all_to_all(regrouped, "rb", split_axis=2, concat_axis=1, tiled=True)
        )
        settled = lax.all_to_all(moved, "rb", split_axis=1, concat_axis=2, tiled=True)
        settled = settled.reshape(2, second_rows, groups_b, first_rows, width_b)
        amplitude = settled.transpose(0, 3, 1, 2, 4).reshape(2, first_rows, second_rows, channels)
    return amplitude


def prop_kernel(turned, n_in, n_out, mat_ref, *refs):
    ins, outs, rest = refs[:n_in], refs[n_in:n_in + n_out], refs[n_in + n_out:]
    depth = mat_ref.shape[1]
    outer = ins[0].shape[1]
    rows = depth // n_out
    step = pl.program_id(0)

    def one(o, carry):
        real = jnp.concatenate([r[0, o] for r in ins], axis=0)
        imag = jnp.concatenate([r[1, o] for r in ins], axis=0)
        res = jnp.dot(
            mat_ref[0], jnp.concatenate([real, imag], axis=1), preferred_element_type=jnp.float32
        ) + jnp.dot(
            mat_ref[1], jnp.concatenate([-imag, real], axis=1), preferred_element_type=jnp.float32
        )
        if turned:
            for p in range(2):
                rest[0][p, pl.ds(step * outer + o, depth, stride=TILE), :] = res[:, p * LANES:(p + 1) * LANES]
        else:
            for p in range(2):
                for s in range(n_out):
                    outs[s][p, o] = res[s * rows:(s + 1) * rows, p * LANES:(p + 1) * LANES].astype(jnp.bfloat16)
        return carry

    lax.fori_loop(0, outer, one, 0)
    if turned:
        @pl.when(step == pl.num_programs(0) - 1)
        def _():
            span = rows * TILE
            for p in range(2):
                for s in range(n_out):
                    outs[s][p] = rest[0][p, s * span:(s + 1) * span, :].reshape(rows, TILE, LANES).astype(jnp.bfloat16)


def propagate(matrix, pieces, place, n_out, turned):
    depth = matrix.shape[1]
    rows = depth // n_out
    outer = 4
    parts = TILE // outer
    in_specs = [pl.BlockSpec(matrix.shape, lambda g: (0, 0, 0))] + [
        pl.BlockSpec((2, outer, p.shape[2], LANES), lambda g: (0, place * parts + g, 0, 0)) for p in pieces
    ]
    if turned:
        shape = (2, rows, TILE, LANES)
        out_specs = [pl.BlockSpec(shape, lambda g: (0, 0, 0, 0))] * n_out
        scratch = [pltpu.VMEM((2, depth * TILE, LANES), jnp.float32)]
    else:
        shape = (2, TILE, rows, LANES)
        out_specs = [pl.BlockSpec((2, outer, rows, LANES), lambda g: (0, g, 0, 0))] * n_out
        scratch = []
    return pl.pallas_call(
        functools.partial(prop_kernel, turned, len(pieces), n_out),
        grid=(parts,),
        in_specs=in_specs,
        out_specs=out_specs,
        out_shape=[jax.ShapeDtypeStruct(shape, jnp.bfloat16)] * n_out,
        scratch_shapes=scratch,
        cost_estimate=pl.CostEstimate(
            flops=8 * depth * depth * TILE * LANES, bytes_accessed=8 * depth * TILE * LANES, transcendentals=0
        ),
        compiler_params=pltpu.CompilerParams(vmem_limit_bytes=56 * 2**20),
    )(matrix, *pieces)


def kick_rows(planes, old, weights, factor):
    coupled = []
    for p in range(2):
        applied = jnp.dot(planes[p], weights, preferred_element_type=jnp.float32)
        total = applied[:, :LANES] * factor[:, 0:1]
        for k in range(1, KTERMS):
            total = total + applied[:, k * LANES:(k + 1) * LANES] * factor[:, k:k + 1]
        coupled.append(total)
    return old[0].astype(jnp.float32) + coupled[1], old[1].astype(jnp.float32) - coupled[0]


def kick_turned_kernel(where_ref, amp_ref, weights_ref, factor_ref, *outs):
    a_rows, b_rows = amp_ref.shape[1], amp_ref.shape[2]
    count = a_rows * b_rows
    planes = [amp_ref[p].reshape(count, amp_ref.shape[3]) for p in range(2)]
    factor = factor_ref[...].reshape(count, KTERMS)
    for s in range(2):
        low = where_ref[1] == s
        old = [jnp.where(low, p[:, :LANES], p[:, LANES:]) for p in planes]
        result = kick_rows(planes, old, weights_ref[s], factor)
        for p in range(2):
            outs[s][p] = jnp.swapaxes(result[p].reshape(a_rows, b_rows, LANES), 0, 1).astype(jnp.bfloat16)


def kick_turned(amplitude, weights, factor, where):
    a_rows, channels = amplitude.shape[1], amplitude.shape[3]
    shape = jax.ShapeDtypeStruct((2, TILE, a_rows, LANES), jnp.bfloat16)
    spec = pltpu.PrefetchScalarGridSpec(
        num_scalar_prefetch=1,
        grid=(a_rows // TILE,),
        in_specs=[
            pl.BlockSpec((2, TILE, TILE, channels), lambda g, w: (0, g, w[0], 0)),
            pl.BlockSpec(weights.shape, lambda g, w: (0, 0, 0)),
            pl.BlockSpec((TILE, TILE, KTERMS), lambda g, w: (g, w[0], 0)),
        ],
        out_specs=[pl.BlockSpec((2, TILE, TILE, LANES), lambda g, w: (0, 0, g, 0))] * 2,
    )
    return pl.pallas_call(
        kick_turned_kernel,
        grid_spec=spec,
        out_shape=[shape, shape],
        cost_estimate=pl.CostEstimate(
            flops=8 * TILE * a_rows * channels * KTERMS * LANES,
            bytes_accessed=8 * TILE * a_rows * channels, transcendentals=0,
        ),
    )(where, amplitude, weights, factor)


def kick_pair_kernel(own_ref, other_ref, weights_ref, factor_ref, own_out, other_out):
    halves = [[ref[p, 0] for p in range(2)] for ref in (own_ref, other_ref)]
    planes = [jnp.concatenate([halves[0][p], halves[1][p]], axis=1) for p in range(2)]
    factor = factor_ref[0]
    for s, out in enumerate((own_out, other_out)):
        result = kick_rows(planes, halves[s], weights_ref[s], factor)
        for p in range(2):
            out[p, 0] = result[p].astype(jnp.bfloat16)


def kick_pair(own, other, weights, factor, place):
    a_rows, b_rows = own.shape[1], own.shape[2]
    block = pl.BlockSpec((2, 1, b_rows, LANES), lambda g: (0, g, 0, 0))
    shape = jax.ShapeDtypeStruct(own.shape, jnp.bfloat16)
    return pl.pallas_call(
        kick_pair_kernel,
        grid=(a_rows,),
        in_specs=[
            block, block,
            pl.BlockSpec(weights.shape, lambda g: (0, 0, 0)),
            pl.BlockSpec((1, b_rows, KTERMS), lambda g: (place * a_rows + g, 0, 0)),
        ],
        out_specs=[block, block],
        out_shape=[shape, shape],
        cost_estimate=pl.CostEstimate(
            flops=4 * a_rows * b_rows * 4 * LANES * KTERMS * LANES,
            bytes_accessed=16 * a_rows * b_rows * LANES, transcendentals=0,
        ),
    )(own, other, weights, factor)


def join_kernel(where_ref, own_ref, other_ref, *refs):
    low = where_ref[1] == 0
    own, other = own_ref[...], other_ref[...]
    refs[-1][:, :, :, :LANES] = jnp.where(low, own, other)
    refs[-1][:, :, :, LANES:] = jnp.where(low, other, own)


def join(own, other, into, where, shape):
    a_rows = own.shape[1]
    step = 32
    have = into is not None
    spec = pltpu.PrefetchScalarGridSpec(
        num_scalar_prefetch=1,
        grid=(a_rows // step,),
        in_specs=[pl.BlockSpec((2, step, TILE, LANES), lambda g, w: (0, g, 0, 0))] * 2
        + ([pl.BlockSpec(memory_space=pl.ANY)] if have else []),
        out_specs=pl.BlockSpec((2, step, TILE, 2 * LANES), lambda g, w: (0, g, w[0], 0)),
    )
    return pl.pallas_call(
        join_kernel,
        grid_spec=spec,
        out_shape=jax.ShapeDtypeStruct(shape, jnp.bfloat16),
        input_output_aliases={3: 0} if have else {},
        cost_estimate=pl.CostEstimate(flops=0, bytes_accessed=8 * own.size, transcendentals=0),
    )(where, own, other, *((into,) if have else ()))


def picks(index):
    full = index.shape[0]
    return (index[:, None] == jnp.arange(full)[None, :]).astype(jnp.bfloat16)


def arranged(matrix, rows, columns):
    first = jnp.einsum("rs,xst->xrt", picks(rows), matrix, preferred_element_type=jnp.float32)
    return jnp.einsum(
        "xrt,ct->xrc", first.astype(jnp.bfloat16), picks(columns), preferred_element_type=jnp.float32
    ).astype(jnp.bfloat16)


def on_device(amplitude, coupling, pattern, radial, first_prop, second_prop):
    a_rows, b_rows, channels = amplitude.shape[1:]
    n_a, n_b = first_prop.shape[1], second_prop.shape[1]
    ra, rb = lax.axis_size("ra"), lax.axis_size("rb")
    far = ra // 2 * rb
    a_far, b_far = n_a // far, n_b // far
    fits = (
        channels == 2 * LANES and ra % 2 == 0 and a_rows % TILE == 0
        and a_far % TILE == 0 and b_far % TILE == 0 and far & (far - 1) == 0
        and far <= 16
    )
    if not fits:
        return plain(amplitude, coupling, pattern, radial, first_prop, second_prop)

    at_a, at_b = lax.axis_index("ra"), lax.axis_index("rb")
    outer, half = at_a // 2, at_a % 2
    spot = outer * rb + at_b
    axes = ("ra", "rb")
    index = lambda ia, ib: ia * rb + ib

    def send_near(piece, s):
        if s == 0:
            return piece
        return lax.ppermute(piece, axes, [(index(i, j), index(i ^ s, j)) for i in range(ra) for j in range(rb)])

    def send_far(piece, s):
        if s == 0:
            return piece
        pairs = []
        for i in range(ra):
            for j in range(rb):
                to = ((i // 2) * rb + j) ^ s
                pairs.append((index(i, j), index((to // rb) * 2 + i % 2, to % rb)))
        return lax.ppermute(piece, axes, pairs)

    half_far, half_rb, half_b = a_far // 2, rb // 2, n_b // 2
    ia, ib = jnp.arange(n_a), jnp.arange(n_b)
    peer = spot ^ (ia // a_far)
    t = ia % a_far
    far_a = (peer // rb) * 2 * a_rows + (t // half_far) * a_rows + (peer % rb) * half_far + t % half_far
    peer = spot ^ (ib // b_far)
    far_b = (peer % rb) * b_rows + (peer // rb) * b_far + ib % b_far
    near_a = (at_a ^ (ia // a_rows)) * a_rows + ia % a_rows
    near_b = (half ^ (ib // half_b)) * half_b + ib % half_b

    first_out = arranged(first_prop, far_a, near_a)
    second_in = arranged(second_prop, near_b, far_b)
    second_out = arranged(second_prop, far_b, near_b)
    first_back = arranged(first_prop, near_a, far_a)

    weights = masked_weights(coupling, pattern).reshape(KTERMS, 2, LANES, channels)
    weights = weights.transpose(1, 3, 0, 2).reshape(2, channels, KTERMS * LANES)
    weights = jnp.where(half == 0, weights, weights[::-1])
    near_radial = radial.transpose(1, 2, 0)

    b_parts, a_parts = b_far // TILE, a_far // TILE

    def block_of(s, part):
        return jnp.stack([(outer ^ s) * b_parts + part, half]).astype(jnp.int32)

    kicks = []
    for part in range(b_parts):
        made = [None] * ra
        for s in reversed(range(ra // 2)):
            made[2 * s], made[2 * s + 1] = kick_turned(amplitude, weights, near_radial, block_of(s, part))
        kicks.append(made)
    later_radial = lax.optimization_barrier((radial, kicks[-1]))[0]

    got = []
    for u in range(rb):
        pairs = []
        for i in range(ra):
            for j in range(rb):
                to = ((i % 2) * half_rb + j % half_rb) ^ u
                pairs.append((index(i, j), index(i // 2 * 2 + j // half_rb, to)))
        to = (half * half_rb + at_b % half_rb) ^ u
        piece = lax.dynamic_slice_in_dim(later_radial, to * half_far, half_far, axis=1)
        got.append(lax.ppermute(piece, axes, pairs))

    halves, held = [], []
    for part in range(b_parts):
        made = kicks[part]
        if part:
            made = lax.optimization_barrier((made, pieces))[0]
        pieces = [send_near(made[s], s) for s in range(ra)]
        spread = propagate(first_out, pieces, 0, far * a_parts, True)
        held.append([spread[p::a_parts] for p in range(a_parts)])
    for p in range(a_parts):
        for part in range(b_parts):
            sent = held[part][p]
            halves.append([send_far(h, s) for s, h in enumerate(sent)])
    halves = [halves[p * b_parts:(p + 1) * b_parts] for p in range(a_parts)]

    turned = weights.reshape(2, 2, LANES, KTERMS * LANES)
    turned = jnp.where(half == 0, turned, turned[:, ::-1]).reshape(weights.shape)
    ordered = jnp.stack(got)
    for bit in range(rb.bit_length() - 1):
        pairs = ordered.reshape(rb >> (bit + 1), 2, 1 << bit, *got[0].shape)
        pairs = jnp.where((at_b >> bit) % 2 == 0, pairs, pairs[:, ::-1])
        ordered = pairs.reshape(rb, *got[0].shape)
    ordered = ordered.reshape(2, half_rb, KTERMS, half_far, b_rows)
    far_radial = ordered.transpose(0, 3, 1, 4, 2).reshape(a_far, half_b, KTERMS)
    back = []
    for part in range(a_parts):
        gathered = [halves[part][q][s] for s in range(far) for q in range(b_parts)]
        own, other = propagate(second_in, gathered, 0, 2, False)
        other = send_near(other, 1)
        own, other = kick_pair(own, other, turned, far_radial, part)
        other = send_near(other, 1)
        spread = propagate(second_out, [own, other], 0, far, True)
        back.append([send_far(h, s) for s, h in enumerate(spread)])
    gathered = [back[part][s] for s in range(far) for part in range(a_parts)]

    result = None
    for part in range(b_parts):
        moved = propagate(first_back, gathered, part, ra, True)
        moved = [send_near(piece, s) for s, piece in enumerate(moved)]
        for s in range(ra // 2):
            result = join(moved[2 * s], moved[2 * s + 1], result, block_of(s, part), amplitude.shape)
    return result


def solution(mesh):
    return jax.shard_map(
        on_device,
        mesh=mesh,
        in_specs=(P(None, "ra", "rb", None), P(), P(), P(None, "ra", "rb"), P(), P()),
        out_specs=P(None, "ra", "rb", None),
        check_vma=False,
    )
```

```python
import functools

import jax
import jax.numpy as jnp
from jax import lax
from jax.experimental import pallas as pl
from jax.experimental.pallas import tpu as pltpu
from jax.sharding import PartitionSpec as P


KTERMS = 6
STEPS = 2
LANES = 128
TILE = 16


def complex_rows(matrix, piece):
    form = "ac,cqw->aqw"
    real_part = jnp.einsum(
        form, matrix[0], piece[0], preferred_element_type=jnp.float32
    ) - jnp.einsum(form, matrix[1], piece[1], preferred_element_type=jnp.float32)
    imag_part = jnp.einsum(
        form, matrix[0], piece[1], preferred_element_type=jnp.float32
    ) + jnp.einsum(form, matrix[1], piece[0], preferred_element_type=jnp.float32)
    return jnp.stack([real_part, imag_part]).astype(jnp.bfloat16)


def masked_weights(coupling, pattern):
    channels = coupling.shape[1]
    count = pattern.shape[1]
    block_size = channels // count
    spread = jnp.broadcast_to(
        pattern[:, :, None, :, None], (KTERMS, count, block_size, count, block_size)
    )
    return coupling * spread.reshape(KTERMS, channels, channels).astype(jnp.bfloat16)


def plain(amplitude, coupling, pattern, radial, first_prop, second_prop):
    first_rows, second_rows, channels = (amplitude.shape[1], amplitude.shape[2], amplitude.shape[3])
    cells = first_rows * second_rows
    groups_a = lax.axis_size("ra")
    groups_b = lax.axis_size("rb")
    width_a = channels // groups_a
    width_b = channels // groups_b
    weights = masked_weights(coupling, pattern)
    radial_cells = radial.reshape(KTERMS, cells).T
    for _ in range(STEPS):
        flat = amplitude.reshape(2 * cells, channels)
        applied = jnp.einsum("mj,kij->mki", flat, weights, preferred_element_type=jnp.float32)
        applied = applied.reshape(2, cells, KTERMS, channels)
        coupled = jnp.sum(applied * radial_cells[None, :, :, None], axis=2)
        wide = amplitude.reshape(2, cells, channels).astype(jnp.float32)
        kicked = jnp.stack([wide[0] + coupled[1], wide[1] - coupled[0]]).astype(jnp.bfloat16)
        grouped = kicked.reshape(2, first_rows, second_rows, groups_a, width_a)
        grouped = grouped.transpose(0, 1, 3, 2, 4).reshape(
            2, first_rows, groups_a, second_rows * width_a
        )
        half = complex_rows(
            first_prop, lax.all_to_all(grouped, "ra", split_axis=2, concat_axis=1, tiled=True)
        )
        restored = lax.all_to_all(half, "ra", split_axis=1, concat_axis=2, tiled=True)
        restored = restored.reshape(2, first_rows, groups_a, second_rows, width_a)
        restored = restored.transpose(0, 1, 3, 2, 4).reshape(
            2, first_rows, second_rows, groups_b, width_b
        )
        regrouped = restored.transpose(0, 2, 3, 1, 4).reshape(
            2, second_rows, groups_b, first_rows * width_b
        )
        moved = complex_rows(
            second_prop, lax.all_to_all(regrouped, "rb", split_axis=2, concat_axis=1, tiled=True)
        )
        settled = lax.all_to_all(moved, "rb", split_axis=1, concat_axis=2, tiled=True)
        settled = settled.reshape(2, second_rows, groups_b, first_rows, width_b)
        amplitude = settled.transpose(0, 3, 1, 2, 4).reshape(2, first_rows, second_rows, channels)
    return amplitude


def prop_kernel(turned, n_in, n_out, mat_ref, *refs):
    ins, outs, rest = refs[:n_in], refs[n_in:n_in + n_out], refs[n_in + n_out:]
    depth = mat_ref.shape[1]
    outer = ins[0].shape[1]
    rows = depth // n_out
    step = pl.program_id(0)

    def one(o, carry):
        real = jnp.concatenate([r[0, o] for r in ins], axis=0)
        imag = jnp.concatenate([r[1, o] for r in ins], axis=0)
        res = jnp.dot(
            mat_ref[0], jnp.concatenate([real, imag], axis=1), preferred_element_type=jnp.float32
        ) + jnp.dot(
            mat_ref[1], jnp.concatenate([-imag, real], axis=1), preferred_element_type=jnp.float32
        )
        if turned:
            for p in range(2):
                rest[0][p, pl.ds(step * outer + o, depth, stride=TILE), :] = res[:, p * LANES:(p + 1) * LANES]
        else:
            for p in range(2):
                for s in range(n_out):
                    outs[s][p, o] = res[s * rows:(s + 1) * rows, p * LANES:(p + 1) * LANES].astype(jnp.bfloat16)
        return carry

    lax.fori_loop(0, outer, one, 0)
    if turned:
        @pl.when(step == pl.num_programs(0) - 1)
        def _():
            span = rows * TILE
            for p in range(2):
                for s in range(n_out):
                    outs[s][p] = rest[0][p, s * span:(s + 1) * span, :].reshape(rows, TILE, LANES).astype(jnp.bfloat16)


def propagate(matrix, pieces, place, n_out, turned):
    depth = matrix.shape[1]
    rows = depth // n_out
    outer = 4
    parts = TILE // outer
    in_specs = [pl.BlockSpec(matrix.shape, lambda g: (0, 0, 0))] + [
        pl.BlockSpec((2, outer, p.shape[2], LANES), lambda g: (0, place * parts + g, 0, 0)) for p in pieces
    ]
    if turned:
        shape = (2, rows, TILE, LANES)
        out_specs = [pl.BlockSpec(shape, lambda g: (0, 0, 0, 0))] * n_out
        scratch = [pltpu.VMEM((2, depth * TILE, LANES), jnp.float32)]
    else:
        shape = (2, TILE, rows, LANES)
        out_specs = [pl.BlockSpec((2, outer, rows, LANES), lambda g: (0, g, 0, 0))] * n_out
        scratch = []
    return pl.pallas_call(
        functools.partial(prop_kernel, turned, len(pieces), n_out),
        grid=(parts,),
        in_specs=in_specs,
        out_specs=out_specs,
        out_shape=[jax.ShapeDtypeStruct(shape, jnp.bfloat16)] * n_out,
        scratch_shapes=scratch,
        cost_estimate=pl.CostEstimate(
            flops=8 * depth * depth * TILE * LANES, bytes_accessed=8 * depth * TILE * LANES, transcendentals=0
        ),
        compiler_params=pltpu.CompilerParams(vmem_limit_bytes=56 * 2**20),
    )(matrix, *pieces)


def kick_rows(planes, old, weights, factor):
    coupled = []
    for p in range(2):
        applied = jnp.dot(planes[p], weights, preferred_element_type=jnp.float32)
        total = applied[:, :LANES] * factor[:, 0:1]
        for k in range(1, KTERMS):
            total = total + applied[:, k * LANES:(k + 1) * LANES] * factor[:, k:k + 1]
        coupled.append(total)
    return old[0].astype(jnp.float32) + coupled[1], old[1].astype(jnp.float32) - coupled[0]


def kick_turned_kernel(where_ref, amp_ref, weights_ref, factor_ref, *outs):
    a_rows, b_rows = amp_ref.shape[1], amp_ref.shape[2]
    count = a_rows * b_rows
    planes = [amp_ref[p].reshape(count, amp_ref.shape[3]) for p in range(2)]
    factor = factor_ref[...].reshape(count, KTERMS)
    for s in range(2):
        low = where_ref[1] == s
        old = [jnp.where(low, p[:, :LANES], p[:, LANES:]) for p in planes]
        result = kick_rows(planes, old, weights_ref[s], factor)
        for p in range(2):
            outs[s][p] = jnp.swapaxes(result[p].reshape(a_rows, b_rows, LANES), 0, 1).astype(jnp.bfloat16)


def kick_turned(amplitude, weights, factor, where):
    a_rows, channels = amplitude.shape[1], amplitude.shape[3]
    shape = jax.ShapeDtypeStruct((2, TILE, a_rows, LANES), jnp.bfloat16)
    spec = pltpu.PrefetchScalarGridSpec(
        num_scalar_prefetch=1,
        grid=(a_rows // TILE,),
        in_specs=[
            pl.BlockSpec((2, TILE, TILE, channels), lambda g, w: (0, g, w[0], 0)),
            pl.BlockSpec(weights.shape, lambda g, w: (0, 0, 0)),
            pl.BlockSpec((TILE, TILE, KTERMS), lambda g, w: (g, w[0], 0)),
        ],
        out_specs=[pl.BlockSpec((2, TILE, TILE, LANES), lambda g, w: (0, 0, g, 0))] * 2,
    )
    return pl.pallas_call(
        kick_turned_kernel,
        grid_spec=spec,
        out_shape=[shape, shape],
        cost_estimate=pl.CostEstimate(
            flops=8 * TILE * a_rows * channels * KTERMS * LANES,
            bytes_accessed=8 * TILE * a_rows * channels, transcendentals=0,
        ),
    )(where, amplitude, weights, factor)


def kick_pair_kernel(own_ref, other_ref, weights_ref, factor_ref, own_out, other_out):
    halves = [[ref[p, 0] for p in range(2)] for ref in (own_ref, other_ref)]
    planes = [jnp.concatenate([halves[0][p], halves[1][p]], axis=1) for p in range(2)]
    factor = factor_ref[0]
    for s, out in enumerate((own_out, other_out)):
        result = kick_rows(planes, halves[s], weights_ref[s], factor)
        for p in range(2):
            out[p, 0] = result[p].astype(jnp.bfloat16)


def kick_pair(own, other, weights, factor, place):
    a_rows, b_rows = own.shape[1], own.shape[2]
    block = pl.BlockSpec((2, 1, b_rows, LANES), lambda g: (0, g, 0, 0))
    shape = jax.ShapeDtypeStruct(own.shape, jnp.bfloat16)
    return pl.pallas_call(
        kick_pair_kernel,
        grid=(a_rows,),
        in_specs=[
            block, block,
            pl.BlockSpec(weights.shape, lambda g: (0, 0, 0)),
            pl.BlockSpec((1, b_rows, KTERMS), lambda g: (place * a_rows + g, 0, 0)),
        ],
        out_specs=[block, block],
        out_shape=[shape, shape],
        cost_estimate=pl.CostEstimate(
            flops=4 * a_rows * b_rows * 4 * LANES * KTERMS * LANES,
            bytes_accessed=16 * a_rows * b_rows * LANES, transcendentals=0,
        ),
    )(own, other, weights, factor)


def join_kernel(where_ref, own_ref, other_ref, *refs):
    low = where_ref[1] == 0
    own, other = own_ref[...], other_ref[...]
    refs[-1][:, :, :, :LANES] = jnp.where(low, own, other)
    refs[-1][:, :, :, LANES:] = jnp.where(low, other, own)


def join(own, other, into, where, shape):
    a_rows = own.shape[1]
    step = 32
    have = into is not None
    spec = pltpu.PrefetchScalarGridSpec(
        num_scalar_prefetch=1,
        grid=(a_rows // step,),
        in_specs=[pl.BlockSpec((2, step, TILE, LANES), lambda g, w: (0, g, 0, 0))] * 2
        + ([pl.BlockSpec(memory_space=pl.ANY)] if have else []),
        out_specs=pl.BlockSpec((2, step, TILE, 2 * LANES), lambda g, w: (0, g, w[0], 0)),
    )
    return pl.pallas_call(
        join_kernel,
        grid_spec=spec,
        out_shape=jax.ShapeDtypeStruct(shape, jnp.bfloat16),
        input_output_aliases={3: 0} if have else {},
        cost_estimate=pl.CostEstimate(flops=0, bytes_accessed=8 * own.size, transcendentals=0),
    )(where, own, other, *((into,) if have else ()))


def picks(index):
    full = index.shape[0]
    return (index[:, None] == jnp.arange(full)[None, :]).astype(jnp.bfloat16)


def arranged(matrix, rows, columns):
    first = jnp.einsum("rs,xst->xrt", picks(rows), matrix, preferred_element_type=jnp.float32)
    return jnp.einsum(
        "xrt,ct->xrc", first.astype(jnp.bfloat16), picks(columns), preferred_element_type=jnp.float32
    ).astype(jnp.bfloat16)


def on_device(amplitude, coupling, pattern, radial, first_prop, second_prop):
    a_rows, b_rows, channels = amplitude.shape[1:]
    n_a, n_b = first_prop.shape[1], second_prop.shape[1]
    ra, rb = lax.axis_size("ra"), lax.axis_size("rb")
    far = ra // 2 * rb
    a_far, b_far = n_a // far, n_b // far
    fits = (
        channels == 2 * LANES and ra % 2 == 0 and a_rows % TILE == 0
        and a_far % TILE == 0 and b_far % TILE == 0 and far & (far - 1) == 0
        and far <= 16
    )
    if not fits:
        return plain(amplitude, coupling, pattern, radial, first_prop, second_prop)

    at_a, at_b = lax.axis_index("ra"), lax.axis_index("rb")
    outer, half = at_a // 2, at_a % 2
    spot = outer * rb + at_b
    axes = ("ra", "rb")
    index = lambda ia, ib: ia * rb + ib

    def send_near(piece, s):
        if s == 0:
            return piece
        return lax.ppermute(piece, axes, [(index(i, j), index(i ^ s, j)) for i in range(ra) for j in range(rb)])

    def send_far(piece, s):
        if s == 0:
            return piece
        pairs = []
        for i in range(ra):
            for j in range(rb):
                to = ((i // 2) * rb + j) ^ s
                pairs.append((index(i, j), index((to // rb) * 2 + i % 2, to % rb)))
        return lax.ppermute(piece, axes, pairs)

    half_far, half_rb, half_b = a_far // 2, rb // 2, n_b // 2
    ia, ib = jnp.arange(n_a), jnp.arange(n_b)
    peer = spot ^ (ia // a_far)
    t = ia % a_far
    far_a = (peer // rb) * 2 * a_rows + (t // half_far) * a_rows + (peer % rb) * half_far + t % half_far
    peer = spot ^ (ib // b_far)
    far_b = (peer % rb) * b_rows + (peer // rb) * b_far + ib % b_far
    near_a = (at_a ^ (ia // a_rows)) * a_rows + ia % a_rows
    near_b = (half ^ (ib // half_b)) * half_b + ib % half_b

    first_out = arranged(first_prop, far_a, near_a)
    second_in = arranged(second_prop, near_b, far_b)
    second_out = arranged(second_prop, far_b, near_b)
    first_back = arranged(first_prop, near_a, far_a)

    weights = masked_weights(coupling, pattern).reshape(KTERMS, 2, LANES, channels)
    weights = weights.transpose(1, 3, 0, 2).reshape(2, channels, KTERMS * LANES)
    weights = jnp.where(half == 0, weights, weights[::-1])
    near_radial = radial.transpose(1, 2, 0)

    b_parts, a_parts = b_far // TILE, a_far // TILE

    def block_of(s, part):
        return jnp.stack([(outer ^ s) * b_parts + part, half]).astype(jnp.int32)

    kicks = []
    for part in range(b_parts):
        made = [None] * ra
        for s in reversed(range(ra // 2)):
            made[2 * s], made[2 * s + 1] = kick_turned(amplitude, weights, near_radial, block_of(s, part))
        kicks.append(made)
    halves = []
    for part in range(b_parts):
        made = kicks[part]
        if part:
            made = lax.optimization_barrier((made, pieces))[0]
        pieces = [send_near(made[s], s) for s in range(ra)]
        spread = propagate(first_out, pieces, 0, far, True)
        halves.append([send_far(h, s) for s, h in enumerate(spread)])
    gathered = [halves[part][s] for s in range(far) for part in range(b_parts)]

    later_radial = lax.optimization_barrier((radial, spread))[0]

    got = []
    for u in range(rb):
        pairs = []
        for i in range(ra):
            for j in range(rb):
                to = ((i % 2) * half_rb + j % half_rb) ^ u
                pairs.append((index(i, j), index(i // 2 * 2 + j // half_rb, to)))
        to = (half * half_rb + at_b % half_rb) ^ u
        piece = lax.dynamic_slice_in_dim(later_radial, to * half_far, half_far, axis=1)
        got.append(lax.ppermute(piece, axes, pairs))

    turned = weights.reshape(2, 2, LANES, KTERMS * LANES)
    turned = jnp.where(half == 0, turned, turned[:, ::-1]).reshape(weights.shape)
    ordered = jnp.stack(got)
    for bit in range(rb.bit_length() - 1):
        pairs = ordered.reshape(rb >> (bit + 1), 2, 1 << bit, *got[0].shape)
        pairs = jnp.where((at_b >> bit) % 2 == 0, pairs, pairs[:, ::-1])
        ordered = pairs.reshape(rb, *got[0].shape)
    ordered = ordered.reshape(2, half_rb, KTERMS, half_far, b_rows)
    far_radial = ordered.transpose(0, 3, 1, 4, 2).reshape(a_far, half_b, KTERMS)
    back = []
    for part in range(a_parts):
        own, other = propagate(second_in, gathered, part, 2, False)
        other = send_near(other, 1)
        own, other = kick_pair(own, other, turned, far_radial, part)
        other = send_near(other, 1)
        spread = propagate(second_out, [own, other], 0, far, True)
        back.append([send_far(h, s) for s, h in enumerate(spread)])
    gathered = [back[part][s] for s in range(far) for part in range(a_parts)]

    result = None
    for part in range(b_parts):
        moved = propagate(first_back, gathered, part, ra, True)
        moved = [send_near(piece, s) for s, piece in enumerate(moved)]
        for s in range(ra // 2):
            result = join(moved[2 * s], moved[2 * s + 1], result, block_of(s, part), amplitude.shape)
    return result


def solution(mesh):
    return jax.shard_map(
        on_device,
        mesh=mesh,
        in_specs=(P(None, "ra", "rb", None), P(), P(), P(None, "ra", "rb"), P(), P()),
        out_specs=P(None, "ra", "rb", None),
        check_vma=False,
    )
```
